32 devices in a mesh: row: 8 (over z, x), col: 2 (over core), rank: 2 (over y).
Axes of the slice: x: 2, y: 2, z: 4, core: 2. Of those that a mesh axis runs over, the one named last changes fastest.
Arguments:
- tensor: bfloat16 [64, 2048, 2048], P(None, 'row', 'col'), may hold values from -6 to 6
- aux_factor: bfloat16 [64, 256], P(None, 'rank'), may hold values from -0.75 to 0.75
- row_factor: bfloat16 [2048, 256], P(('row', 'col'), 'rank'), may hold values from -0.125 to 0.125
- col_factor: bfloat16 [2048, 256], P(('col', 'row'), 'rank'), may hold values from -0.125 to 0.125
Outputs:
- row_result: float32 [2048, 256], P(('row', 'col'), 'rank')
- aux_result: float32 [64, 256], P('row', 'rank')
The draws below stay inside these ranges and needn't reach their ends.
All inputs are finite; a program needn't handle non-finite values.
Results may differ from the reference program's by a relative error of at most 0.0003.
Values may be sent and summed in bfloat16 or wider, within the bound.
A program may use at most 128 MiB of HBM per device.

```python
import jax
import jax.numpy as jnp
from jax import lax

AUX = 64
ORB_ROW = 2048
ORB_COL = 2048
RANK = 256


def block_levels(key, shape, split, smallest, top_value):
    def one(position, blocks):
        steps = jax.random.uniform(jax.random.fold_in(jax.random.fold_in(key, 6), position), (blocks,), jnp.float32, smallest / len(split), top_value / len(split))
        return jnp.repeat(jnp.exp(steps), shape[position] // blocks).reshape((-1,) + (1,) * (len(shape) - position - 1))

    gain = one(*split[0])
    for cut in split[1:]:
        gain = gain * one(*cut)
    return gain


def gaussian(stream_key, dims, width, bound, cuts=(), held_as=jnp.bfloat16):
    entries = width * jax.random.normal(stream_key, dims, jnp.float32)
    if cuts:
        entries = entries * block_levels(stream_key, dims, cuts, -0.22, 0.18)
    return jnp.clip(entries, -bound, bound).astype(held_as)


def setup_inputs(seed: int = 0) -> dict:
    arg_keys = jax.random.split(jax.random.key(seed), 5)
    return {
        "tensor": gaussian(arg_keys[0], (AUX, ORB_ROW, ORB_COL), 1.0, 6.0, ((1, 8), (2, 2))),
        "aux_factor": gaussian(arg_keys[1], (AUX, RANK), AUX ** -0.5, 0.75, ((1, 2),)),
        "row_factor": gaussian(arg_keys[2], (ORB_ROW, RANK), ORB_ROW ** -0.5, 0.125, ((0, 16), (1, 2))),
        "col_factor": gaussian(arg_keys[3], (ORB_COL, RANK), ORB_COL ** -0.5, 0.125, ((0, 16), (1, 2))),
    }


def reference(tensor, aux_factor, row_factor, col_factor):
    columns = col_factor.astype(jnp.float32)
    row_panel = row_factor.astype(jnp.float32)
    aux_panel = aux_factor.astype(jnp.float32)
    row_total = jnp.zeros((ORB_ROW, RANK), jnp.float32)
    pieces = []
    for start in range(0, AUX, 8):
        slab = tensor[start:start + 8].astype(jnp.float32)
        product = jnp.dot(slab.reshape(8 * ORB_ROW, ORB_COL), columns, precision=lax.Precision.HIGHEST).reshape(8, ORB_ROW, RANK)
        row_total = row_total + jnp.sum(product * aux_panel[start:start + 8][:, None, :], axis=0)
        pieces.append(jnp.sum(product * row_panel[None, :, :], axis=1))
    return row_total, jnp.concatenate(pieces, axis=0)
```

```python
import functools

import jax
import jax.numpy as jnp
from jax import lax
from jax.experimental import pallas as pl
from jax.experimental.pallas import tpu as pltpu
from jax.sharding import PartitionSpec as P

MESH = pl.DeviceIdType.MESH
f32 = jnp.float32


def kernel(R, C, tensor, aux, rowf, colf, row_out, aux_out,
           tbuf, colbuf, rowbuf, auxbuf, row_panel, aux_panel, row_acc, aux_acc, row_in, aux_in,
           t_sem, c_send, c_recv, r_send, r_recv, l_sem, a_send, a_recv, p_send, p_recv):
    r = lax.axis_index("row")
    c = lax.axis_index("col")
    other = 1 - c
    A, I, J = tensor.shape
    N = colf.shape[1]
    jb = colf.shape[0]
    ib = rowf.shape[0]
    ac = A // R
    H = R // 2
    jh = J // 2
    half = r // H

    def chunk_of(s):
        return lax.rem(r + 1 + s, R)

    def load(p, s):
        k = chunk_of(s)
        h = half if p == 0 else 1 - half
        cols = pl.ds(pl.multiple_of(h * jh, jh), jh)
        return pltpu.make_async_copy(
            tensor.at[pl.ds(k * ac, ac), :, cols], tbuf.at[p, k], t_sem.at[p, s])

    own_col = pltpu.make_async_copy(colf, colbuf.at[r], l_sem.at[0])
    own_row = pltpu.make_async_copy(rowf, rowbuf.at[c], l_sem.at[1])
    own_aux = pltpu.make_async_copy(aux, auxbuf, l_sem.at[2])
    own_col.start()
    own_row.start()
    own_aux.start()

    barrier = pltpu.get_barrier_semaphore()
    for d in range(R):
        for e in range(C):
            if d or e:
                pl.semaphore_signal(
                    barrier, inc=1, device_id={"row": lax.rem(r + d, R), "col": lax.rem(c + e, C)},
                    device_id_type=MESH)
    for p in range(2):
        for s in range(R):
            load(p, s).start()
    pl.semaphore_wait(barrier, R * C - 1)

    def col_copy(target):
        return pltpu.make_async_remote_copy(
            src_ref=colf, dst_ref=colbuf.at[r], send_sem=c_send.at[target], recv_sem=c_recv.at[r],
            device_id={"row": target}, device_id_type=MESH)

    def col_arrival(source):
        return pltpu.make_async_remote_copy(
            src_ref=colf, dst_ref=colbuf.at[source], send_sem=c_send.at[source], recv_sem=c_recv.at[source],
            device_id={"row": source}, device_id_type=MESH)

    near = [half * H + lax.rem(lax.rem(r, H) + d, H) for d in range(1, H)]
    far = [(1 - half) * H + lax.rem(lax.rem(r, H) + d, H) for d in range(H)]
    for target in near:
        col_copy(target).start()
    row_copy = pltpu.make_async_remote_copy(
        src_ref=rowf, dst_ref=rowbuf.at[c], send_sem=r_send, recv_sem=r_recv,
        device_id={"col": other}, device_id_type=MESH)
    row_copy.start()
    for target in far:
        col_copy(target).start()

    row_acc[...] = jnp.zeros_like(row_acc)
    own_aux.wait()
    aux_panel[...] = auxbuf[...].astype(f32).reshape(R, ac, N)
    own_row.wait()
    row_copy.wait()
    row_panel[...] = rowbuf[...].reshape(C * ib, N).astype(f32)
    own_col.wait()
    for source in near:
        col_arrival(source).wait_recv()

    def block(p, s):
        load(p, s).wait()
        k = chunk_of(s)
        h = half if p == 0 else 1 - half
        weights = colbuf[pl.ds(h * H, H)].reshape(H * jb, N)
        inner = jnp.dot(tbuf[p, k].reshape(ac * I, jh), weights, preferred_element_type=f32).reshape(ac, I, N)
        row_acc[...] += jnp.sum(inner * aux_panel[k][:, None, :], axis=0)
        part = jnp.sum(inner * row_panel[...][None], axis=1)
        if p == 0:
            aux_acc[k] = part
        else:
            aux_acc[k] += part
        return k

    def aux_copy(k, e):
        return pltpu.make_async_remote_copy(
            src_ref=aux_acc.at[k], dst_ref=aux_in.at[r, c], send_sem=a_send.at[k, e], recv_sem=a_recv.at[r, c],
            device_id={"row": k, "col": e}, device_id_type=MESH)

    def aux_arrival(source, e):
        return pltpu.make_async_remote_copy(
            src_ref=aux_acc.at[source], dst_ref=aux_in.at[source, e], send_sem=a_send.at[source, e],
            recv_sem=a_recv.at[source, e], device_id={"row": source, "col": e}, device_id_type=MESH)

    def first(s, _):
        block(0, s)
        return 0

    lax.fori_loop(0, R, first, 0)
    for source in far:
        col_arrival(source).wait_recv()

    def second(s, _):
        k = block(1, s)
        aux_copy(k, c).start()
        aux_copy(k, other).start()
        return 0

    lax.fori_loop(0, R - 1, second, 0)
    block(1, R - 1)
    part_copy = pltpu.make_async_remote_copy(
        src_ref=row_acc.at[pl.ds(other * ib, ib)], dst_ref=row_in, send_sem=p_send, recv_sem=p_recv,
        device_id={"col": other}, device_id_type=MESH)
    part_copy.start()
    aux_copy(r, other).start()
    aux_in[r, c] = aux_acc[r]
    for d in range(1, R):
        source = lax.rem(r + d, R)
        for e in range(C):
            aux_arrival(source, e).wait_recv()
    aux_arrival(r, other).wait_recv()
    aux_out[...] = jnp.sum(aux_in[...].reshape(R * C, ac, N), axis=0)
    part_copy.wait_recv()
    row_out[...] = row_acc[pl.ds(c * ib, ib)] + row_in[...]

    part_copy.wait_send()
    aux_copy(r, other).wait_send()
    for d in range(1, R):
        k = lax.rem(r + d, R)
        col_copy(k).wait_send()
        for e in range(C):
            aux_copy(k, e).wait_send()


def fused(R, C, tensor, aux, rowf, colf):
    A, I, J = tensor.shape
    jb, N = colf.shape
    ib = rowf.shape[0]
    ac = A // R
    bf16 = tensor.dtype
    anywhere = pl.BlockSpec(memory_space=pltpu.HBM)
    vmem = pl.BlockSpec(memory_space=pltpu.VMEM)
    dma = pltpu.SemaphoreType.DMA
    return pl.pallas_call(
        functools.partial(kernel, R, C),
        out_shape=(jax.ShapeDtypeStruct((ib, N), f32), jax.ShapeDtypeStruct((ac, N), f32)),
        in_specs=[anywhere] * 4,
        out_specs=(vmem, vmem),
        scratch_shapes=[
            pltpu.VMEM((2, R, ac, I, J // 2), bf16),
            pltpu.VMEM((R, jb, N), bf16),
            pltpu.VMEM((C, ib, N), bf16),
            pltpu.VMEM((A, N), bf16),
            pltpu.VMEM((C * ib, N), f32),
            pltpu.VMEM((R, ac, N), f32),
            pltpu.VMEM((C * ib, N), f32),
            pltpu.VMEM((R, ac, N), f32),
            pltpu.VMEM((ib, N), f32),
            pltpu.VMEM((R, C, ac, N), f32),
            dma((2, R)), dma((R,)), dma((R,)), dma, dma, dma((3,)),
            dma((R, C)), dma((R, C)), dma, dma,
        ],
        compiler_params=pltpu.CompilerParams(
            collective_id=0, has_side_effects=True, vmem_limit_bytes=58 * 2**20),
    )(tensor, aux, rowf, colf)


def plain(tensor, aux_factor, row_factor, col_factor):
    row_panel = lax.all_gather(row_factor, "col", axis=0, tiled=True).astype(f32)
    columns = lax.all_gather(col_factor, "row", axis=0, tiled=True)
    A, I, J = tensor.shape
    inner = jnp.dot(tensor.reshape(A * I, J), columns, preferred_element_type=f32).reshape(A, I, -1)
    row_total = jnp.sum(inner * aux_factor.astype(f32)[:, None, :], axis=0)
    aux_total = jnp.sum(inner * row_panel[None], axis=1)
    row_result = lax.psum_scatter(row_total, "col", scatter_dimension=0, tiled=True)
    scattered = lax.psum_scatter(aux_total, "row", scatter_dimension=0, tiled=True)
    return row_result, lax.psum(scattered, "col")


def solution(mesh):
    R, C = mesh.shape["row"], mesh.shape["col"]

    def body(tensor, aux, rowf, colf):
        A, I, J = tensor.shape
        jb, N = colf.shape
        ib = rowf.shape[0]
        fits = (C == 2 and R % 2 == 0 and A % (8 * R) == 0 and ib % 16 == 0 and jb % 16 == 0
                and J % 256 == 0 and N % 128 == 0 and 2 * tensor.size < 48 * 2**20)
        if fits:
            return tuple(fused(R, C, tensor, aux, rowf, colf))
        return plain(tensor, aux, rowf, colf)

    return jax.shard_map(
        body,
        mesh=mesh,
        in_specs=(
            P(None, "row", "col"),
            P(None, "rank"),
            P(("row", "col"), "rank"),
            P(("col", "row"), "rank"),
        ),
        out_specs=(P(("row", "col"), "rank"), P("row", "rank")),
        check_vma=False,
    )
```

```python
import functools

import jax
import jax.numpy as jnp
from jax import lax
from jax.experimental import pallas as pl
from jax.experimental.pallas import tpu as pltpu
from jax.sharding import PartitionSpec as P

MESH = pl.DeviceIdType.MESH
f32 = jnp.float32


def kernel(R, C, tensor, aux, rowf, colf, out,
           tbuf, colbuf, rowbuf, auxbuf, row_panel, aux_panel, row_acc, aux_acc, inner_acc, row_in, aux_in,
           t_sem, c_send, c_recv, r_send, r_recv, l_sem, a_send, a_recv, p_send, p_recv, far_sem):
    r = lax.axis_index("row")
    c = lax.axis_index("col")
    other = 1 - c
    A, I, J = tensor.shape
    N = colf.shape[1]
    jb = colf.shape[0]
    ib = rowf.shape[0]
    ac = A // R
    H = R // 2
    jh = J // 2
    half = r // H

    def chunk_of(s):
        return lax.rem(r + 1 + s, R)

    def load(p, s):
        k = chunk_of(s)
        h = half if p == 0 else 1 - half
        cols = pl.ds(pl.multiple_of(h * jh, jh), jh)
        return pltpu.make_async_copy(
            tensor.at[pl.ds(k * ac, ac), :, cols], tbuf.at[p, k], t_sem.at[p, s])

    own_col = pltpu.make_async_copy(colf, colbuf.at[r], l_sem.at[0])
    own_row = pltpu.make_async_copy(rowf, rowbuf.at[c], l_sem.at[1])
    own_aux = pltpu.make_async_copy(aux, auxbuf, l_sem.at[2])
    own_col.start()
    own_row.start()
    own_aux.start()

    barrier = pltpu.get_barrier_semaphore()
    near = [half * H + lax.rem(lax.rem(r, H) + d, H) for d in range(1, H)]
    far = [(1 - half) * H + lax.rem(lax.rem(r, H) + d, H) for d in range(H)]
    x = lax.rem(r, 2)
    gate = jnp.where(half == 0, H - 2, H) + x
    beyond = jnp.where(half == 0, H, H - 2) + x
    at_gate = r == gate

    def signal(sem, where):
        pl.semaphore_signal(sem, inc=1, device_id=where, device_id_type=MESH)

    signal(barrier, {"col": other})
    for target in near:
        signal(barrier, {"row": target})

    @pl.when(at_gate)
    def _():
        signal(barrier, {"row": beyond})

    for p in range(2):
        for s in range(R):
            load(p, s).start()
    pl.semaphore_wait(barrier, H + jnp.where(at_gate, 1, 0))

    def col_copy(target):
        return pltpu.make_async_remote_copy(
            src_ref=colf, dst_ref=colbuf.at[r], send_sem=c_send.at[target], recv_sem=c_recv.at[r],
            device_id={"row": target}, device_id_type=MESH)

    def col_arrival(source):
        return pltpu.make_async_remote_copy(
            src_ref=colf, dst_ref=colbuf.at[source], send_sem=c_send.at[source], recv_sem=c_recv.at[source],
            device_id={"row": source}, device_id_type=MESH)

    for target in near:
        col_copy(target).start()
    row_copy = pltpu.make_async_remote_copy(
        src_ref=rowf, dst_ref=rowbuf.at[c], send_sem=r_send, recv_sem=r_recv,
        device_id={"col": other}, device_id_type=MESH)
    row_copy.start()

    @pl.when(at_gate)
    def _():
        signal(far_sem, {"row": beyond})

    pl.semaphore_wait(far_sem, 1)

    @pl.when(at_gate)
    def _():
        for d in range(1, H // 2):
            signal(far_sem, {"row": half * H + lax.rem(lax.rem(r, H) + 2 * d, H)})

    for target in far:
        col_copy(target).start()

    row_acc[...] = jnp.zeros_like(row_acc)
    own_aux.wait()
    aux_panel[...] = auxbuf[...].astype(f32).reshape(R, ac, N)
    own_row.wait()
    row_copy.wait()
    row_panel[...] = rowbuf[...].reshape(C * ib, N).astype(f32)
    own_col.wait()
    for source in near:
        col_arrival(source).wait_recv()

    def product(p, s):
        load(p, s).wait()
        k = chunk_of(s)
        h = half if p == 0 else 1 - half
        weights = colbuf[pl.ds(h * H, H)].reshape(H * jb, N)
        return k, jnp.dot(tbuf[p, k].reshape(ac * I, jh), weights, preferred_element_type=f32)

    def block(s):
        k, inner = product(1, s)
        inner = (inner_acc[k] + inner).reshape(ac, I, N)
        row_acc[...] += jnp.sum(inner * aux_panel[k][:, None, :], axis=0)
        aux_acc[k] = jnp.sum(inner * row_panel[...][None], axis=1)
        return k

    def aux_copy(k, e):
        return pltpu.make_async_remote_copy(
            src_ref=aux_acc.at[k], dst_ref=aux_in.at[r, c], send_sem=a_send.at[k, e], recv_sem=a_recv.at[r, c],
            device_id={"row": k, "col": e}, device_id_type=MESH)

    def aux_arrival(source, e):
        return pltpu.make_async_remote_copy(
            src_ref=aux_acc.at[source], dst_ref=aux_in.at[source, e], send_sem=a_send.at[source, e],
            recv_sem=a_recv.at[source, e], device_id={"row": source, "col": e}, device_id_type=MESH)

    def first(s, _):
        k, inner = product(0, s)
        inner_acc[k] = inner
        return 0

    lax.fori_loop(0, R, first, 0)
    for source in far:
        col_arrival(source).wait_recv()

    def second(s, _):
        k = block(s)
        aux_copy(k, c).start()
        aux_copy(k, other).start()
        return 0

    lax.fori_loop(0, R - 1, second, 0)
    block(R - 1)
    part_copy = pltpu.make_async_remote_copy(
        src_ref=row_acc.at[pl.ds(other * ib, ib)], dst_ref=row_in, send_sem=p_send, recv_sem=p_recv,
        device_id={"col": other}, device_id_type=MESH)
    part_copy.start()
    aux_copy(r, other).start()
    aux_in[r, c] = aux_acc[r]
    for d in range(1, R):
        source = lax.rem(r + d, R)
        for e in range(C):
            aux_arrival(source, e).wait_recv()
    aux_arrival(r, other).wait_recv()
    out[ib:, :] = jnp.sum(aux_in[...].reshape(R * C, ac, N), axis=0)
    part_copy.wait_recv()
    out[:ib, :] = row_acc[pl.ds(c * ib, ib)] + row_in[...]

    part_copy.wait_send()
    aux_copy(r, other).wait_send()
    for d in range(1, R):
        k = lax.rem(r + d, R)
        col_copy(k).wait_send()
        for e in range(C):
            aux_copy(k, e).wait_send()


def split(both, row_out, aux_out):
    rows = row_out.shape[0]
    row_out[...] = both[:rows, :]
    aux_out[...] = both[rows:, :]


def fused(R, C, tensor, aux, rowf, colf):
    A, I, J = tensor.shape
    jb, N = colf.shape
    ib = rowf.shape[0]
    ac = A // R
    bf16 = tensor.dtype
    anywhere = pl.BlockSpec(memory_space=pltpu.HBM)
    vmem = pl.BlockSpec(memory_space=pltpu.VMEM)
    dma = pltpu.SemaphoreType.DMA
    both = pl.pallas_call(
        functools.partial(kernel, R, C),
        out_shape=jax.ShapeDtypeStruct((ib + ac, N), f32),
        in_specs=[anywhere] * 4,
        out_specs=vmem,
        scratch_shapes=[
            pltpu.VMEM((2, R, ac, I, J // 2), bf16),
            pltpu.VMEM((R, jb, N), bf16),
            pltpu.VMEM((C, ib, N), bf16),
            pltpu.VMEM((A, N), bf16),
            pltpu.VMEM((C * ib, N), f32),
            pltpu.VMEM((R, ac, N), f32),
            pltpu.VMEM((C * ib, N), f32),
            pltpu.VMEM((R, ac, N), f32),
            pltpu.VMEM((R, ac * I, N), f32),
            pltpu.VMEM((ib, N), f32),
            pltpu.VMEM((R, C, ac, N), f32),
            dma((2, R)), dma((R,)), dma((R,)), dma, dma, dma((3,)),
            dma((R, C)), dma((R, C)), dma, dma, pltpu.SemaphoreType.REGULAR,
        ],
        compiler_params=pltpu.CompilerParams(
            collective_id=0, has_side_effects=True, vmem_limit_bytes=56 * 2**20),
    )(tensor, aux, rowf, colf)
    return pl.pallas_call(
        split,
        out_shape=(jax.ShapeDtypeStruct((ib, N), f32), jax.ShapeDtypeStruct((ac, N), f32)),
        in_specs=[vmem],
        out_specs=(vmem, vmem),
    )(both)


def plain(tensor, aux_factor, row_factor, col_factor):
    row_panel = lax.all_gather(row_factor, "col", axis=0, tiled=True).astype(f32)
    columns = lax.all_gather(col_factor, "row", axis=0, tiled=True)
    A, I, J = tensor.shape
    inner = jnp.dot(tensor.reshape(A * I, J), columns, preferred_element_type=f32).reshape(A, I, -1)
    row_total = jnp.sum(inner * aux_factor.astype(f32)[:, None, :], axis=0)
    aux_total = jnp.sum(inner * row_panel[None], axis=1)
    row_result = lax.psum_scatter(row_total, "col", scatter_dimension=0, tiled=True)
    scattered = lax.psum_scatter(aux_total, "row", scatter_dimension=0, tiled=True)
    return row_result, lax.psum(scattered, "col")


def solution(mesh):
    R, C = mesh.shape["row"], mesh.shape["col"]

    def body(tensor, aux, rowf, colf):
        A, I, J = tensor.shape
        jb, N = colf.shape
        ib = rowf.shape[0]
        fits = (C == 2 and R % 4 == 0 and A % (8 * R) == 0 and ib % 16 == 0 and jb % 16 == 0
                and J % 256 == 0 and N % 128 == 0 and 2 * tensor.size < 36 * 2**20)
        if fits:
            return tuple(fused(R, C, tensor, aux, rowf, colf))
        return plain(tensor, aux, rowf, colf)

    return jax.shard_map(
        body,
        mesh=mesh,
        in_specs=(
            P(None, "row", "col"),
            P(None, "rank"),
            P(("row", "col"), "rank"),
            P(("col", "row"), "rank"),
        ),
        out_specs=(P(("row", "col"), "rank"), P("row", "rank")),
        check_vma=False,
    )
```
